32 devices in a mesh: wide: 8 (over z, x), ffn: 4 (over y, core).
Axes of the slice: x: 2, y: 2, z: 4, core: 2. Of those that a mesh axis runs over, the one named last changes fastest.
Arguments:
- hidden_in: bfloat16 [8192, 1024], P(('wide', 'ffn')), may hold values from -6 to 6
- doc_ids: int32 [8192], P(('wide', 'ffn')), may hold values from -1 to 3, as said below
- out_grad: bfloat16 [8192, 1024], P(('wide', 'ffn')), may hold values from -6 to 6
- w_query: bfloat16 [1024, 1024], P(('wide', 'ffn')), may hold values from -0.25 to 0.25
- b_query: bfloat16 [1024], P(('wide', 'ffn')), may hold values from -1.1953125 to 1.1953125
- w_key: bfloat16 [1024, 1024], P(('wide', 'ffn')), may hold values from -0.25 to 0.25
- w_value: bfloat16 [1024, 1024], P(('wide', 'ffn')), may hold values from -0.1875 to 0.1875
- b_value: bfloat16 [1024], P(('wide', 'ffn')), may hold values from -1.1953125 to 1.1953125
- w_output: bfloat16 [1024, 1024], P(('wide', 'ffn')), may hold values from -0.75 to 0.75
- b_output: bfloat16 [1024], P(('wide', 'ffn')), may hold values from -1.1953125 to 1.1953125
- attn_gain: bfloat16 [1024], P(('wide', 'ffn')), may hold values from 0.25 to 1.75
- attn_shift: bfloat16 [1024], P(('wide', 'ffn')), may hold values from -1.1953125 to 1.1953125
- w_up: bfloat16 [1024, 4096], P('wide', 'ffn'), may hold values from -0.1875 to 0.1875
- b_up: bfloat16 [4096], P(('wide', 'ffn')), may hold values from -1.1953125 to 1.1953125
- w_down: bfloat16 [4096, 1024], P('ffn', 'wide'), may hold values from -0.09375 to 0.09375
- b_down: bfloat16 [1024], P(('wide', 'ffn')), may hold values from -1.1953125 to 1.1953125
- ffn_gain: bfloat16 [1024], P(('wide', 'ffn')), may hold values from 0.25 to 1.75
- ffn_shift: bfloat16 [1024], P(('wide', 'ffn')), may hold values from -1.1953125 to 1.1953125
Outputs:
- out_rows: bfloat16 [8192, 1024], P(('wide', 'ffn'))
- grad_input: float32 [8192, 1024], P(('wide', 'ffn'))
- grad_w_query: float32 [1024, 1024], P(('wide', 'ffn'))
- grad_b_query: float32 [1024], P(('wide', 'ffn'))
- grad_w_key: float32 [1024, 1024], P(('wide', 'ffn'))
- grad_w_value: float32 [1024, 1024], P(('wide', 'ffn'))
- grad_b_value: float32 [1024], P(('wide', 'ffn'))
- grad_w_output: float32 [1024, 1024], P(('wide', 'ffn'))
- grad_b_output: float32 [1024], P(('wide', 'ffn'))
- grad_attn_gain: float32 [1024], P(('wide', 'ffn'))
- grad_attn_shift: float32 [1024], P(('wide', 'ffn'))
- grad_w_up: float32 [1024, 4096], P('wide', 'ffn')
- grad_b_up: float32 [4096], P(('wide', 'ffn'))
- grad_w_down: float32 [4096, 1024], P('ffn', 'wide')
- grad_b_down: float32 [1024], P(('wide', 'ffn'))
- grad_ffn_gain: float32 [1024], P(('wide', 'ffn'))
- grad_ffn_shift: float32 [1024], P(('wide', 'ffn'))
The draws below stay inside these ranges and needn't reach their ends.
Inputs may be any that keep to these rules, and one draw needn't show every extreme that they name: `doc_ids`: within each device's 256 rows either all rows are item 0 (one item of 256 residues), or items 0 to c - 1 of 64 residues each fill the first c * 64 rows for some c of 1 to 4 and the remaining rows are -1. In every draw some device holds one full item and some device holds four short ones.
All inputs are finite; a program needn't handle non-finite values.
Results may differ from the reference program's by a relative error of at most 0.015.
The reference program's roundings to bfloat16 on the way count: a program that leaves them out, or rounds other values in their place, can miss the bound.
Values may be sent and summed in bfloat16 or wider, within the bound.
No kernel may reach another device: no remote copies, remote signals or barrier semaphores. Data moves between devices by JAX's collectives and lax.ppermute only.
A program may use at most 128 MiB of HBM per device.

```python
import math
import jax
import jax.numpy as jnp
from jax import lax

D = 1024
HEADS = 16
FF = 4096
ROWS = 256
HEAD_DIM = 64
SHORT = 64
BLOCKS = 32
TOKENS = 8192


def draw_doc_ids(key, part):
    kind_key, pick_key = jax.random.split(key)
    block_kinds = jax.random.randint(kind_key, (BLOCKS,), 0, 5)
    chosen = jax.random.randint(pick_key, (), 0, BLOCKS)
    block_index = jnp.arange(BLOCKS)
    block_kinds = jnp.where(block_index == chosen, 0, block_kinds)
    block_kinds = jnp.where(block_index == (chosen + 1) % BLOCKS, 4, block_kinds)
    item_number = jnp.arange(ROWS) // SHORT
    short_table = jnp.where(item_number[None, :] < block_kinds[:, None], item_number[None, :], -1)
    id_table = jnp.where(block_kinds[:, None] == 0, 0, short_table)
    return id_table.reshape(TOKENS).astype(jnp.int32)


def level_of(rng, shape, shards, least, largest):
    level = 1.0
    for position, shards_of in shards:
        draws = jax.random.uniform(jax.random.fold_in(jax.random.fold_in(rng, 6), position), (shards_of,), jnp.float32, least / len(shards), largest / len(shards))
        level = level * jnp.repeat(jnp.exp(draws), shape[position] // shards_of).reshape((-1,) + (1,) * (len(shape) - 1 - position))
    return level


def gaussian(key, dims, width, most, cuts=(), held_as=jnp.bfloat16):
    array = jax.random.normal(key, dims, jnp.float32) * width
    if len(cuts) > 0:
        array = level_of(key, dims, cuts, -0.22, 0.18) * array
    return jnp.clip(array, min=-most, max=most).astype(held_as)


def setup_inputs(seed: int = 0) -> dict:
    key_of = jax.random.split(jax.random.key(seed), 19)
    hidden_in = gaussian(key_of[0], (TOKENS, D), 1.0, 6.0, ((0, 32),))
    doc_ids = draw_doc_ids(jax.random.fold_in(key_of[18], 71), 0)
    out_grad = gaussian(key_of[2], (TOKENS, D), 1.0, 6.0, ((0, 32),))
    w_query = gaussian(key_of[3], (D, D), (D // 2) ** -0.5, 0.25, ((0, 32),))
    b_query = gaussian(key_of[4], (D,), 0.3, 1.1953125, ((0, 32),))
    w_key = gaussian(key_of[5], (D, D), (D // 2) ** -0.5, 0.25, ((0, 32),))
    w_value = gaussian(key_of[6], (D, D), D ** -0.5, 0.1875, ((0, 32),))
    b_value = gaussian(key_of[7], (D,), 0.3, 1.1953125, ((0, 32),))
    w_output = gaussian(key_of[8], (D, D), (D // 16) ** -0.5, 0.75, ((0, 32),))
    b_output = gaussian(key_of[9], (D,), 0.3, 1.1953125, ((0, 32),))
    attn_gain = jnp.clip(1.0 + 0.15 * jax.random.normal(key_of[10], (D,), jnp.float32), 0.25, 1.75).astype(jnp.bfloat16)
    attn_shift = gaussian(key_of[11], (D,), 0.3, 1.1953125, ((0, 32),))
    w_up = gaussian(key_of[12], (D, FF), D ** -0.5, 0.1875, ((0, 8), (1, 4)))
    b_up = gaussian(key_of[13], (FF,), 0.3, 1.1953125, ((0, 32),))
    w_down = gaussian(key_of[14], (FF, D), FF ** -0.5, 0.09375, ((0, 4), (1, 8)))
    b_down = gaussian(key_of[15], (D,), 0.3, 1.1953125, ((0, 32),))
    ffn_gain = jnp.clip(1.0 + 0.15 * jax.random.normal(key_of[16], (D,), jnp.float32), 0.25, 1.75).astype(jnp.bfloat16)
    ffn_shift = gaussian(key_of[17], (D,), 0.3, 1.1953125, ((0, 32),))
    return {"hidden_in": hidden_in, "doc_ids": doc_ids, "out_grad": out_grad, "w_query": w_query, "b_query": b_query, "w_key": w_key, "w_value": w_value, "b_value": b_value, "w_output": w_output, "b_output": b_output, "attn_gain": attn_gain, "attn_shift": attn_shift, "w_up": w_up, "b_up": b_up, "w_down": w_down, "b_down": b_down, "ffn_gain": ffn_gain, "ffn_shift": ffn_shift}


@jax.custom_vjp
def low(v):
    return lax.optimization_barrier(v.astype(jnp.bfloat16)).astype(jnp.float32)

@jax.custom_vjp
def low_back(v):
    return v

def low_keep(v):
    return (low(v), None)

def low_pass(kept, grad):
    return (grad,)

def back_keep(v):
    return (v, None)

def back_low(kept, grad):
    return (low(grad),)
low.defvjp(low_keep, low_pass)
low_back.defvjp(back_keep, back_low)
norm_eps = 1e-12
highest = lax.Precision.HIGHEST

def matmul(left, right):
    return jnp.dot(left, right, precision=highest, preferred_element_type=jnp.float32)

def layer_norm(values, gain, shift):
    centre = values - lax.optimization_barrier(jnp.mean(values, axis=-1, keepdims=True))
    inverse = lax.rsqrt(lax.optimization_barrier(jnp.mean(centre * centre, axis=-1, keepdims=True)) + norm_eps)
    return centre * inverse * gain + shift

def gelu_exact(values):
    return 0.5 * values * (1.0 + jax.scipy.special.erf(values * (1.0 / math.sqrt(2.0))))

def block_layer(params, inputs, block_ids):
    w_query, b_query, w_key, w_value, b_value, w_output, b_output, attn_gain, attn_shift, w_up, b_up, w_down, b_down, ffn_gain, ffn_shift = params
    row_count = inputs.shape[0]
    queries = low(low_back(matmul(inputs, w_query) + b_query)).reshape(row_count, HEADS, HEAD_DIM)
    key_rows = low(low_back(matmul(inputs, w_key))).reshape(row_count, HEADS, HEAD_DIM)
    value_rows = low(low_back(matmul(inputs, w_value) + b_value)).reshape(row_count, HEADS, HEAD_DIM)
    scores = jnp.einsum('qhd,khd->hqk', queries, key_rows, precision=highest) * HEAD_DIM ** (-0.5)
    allowed = block_ids[:, None] == block_ids[None, :]
    scores = low_back(jnp.where(allowed[None, :, :], scores, -1000000000.0))
    top_score = lax.optimization_barrier(jnp.max(scores, axis=-1, keepdims=True))
    expo_terms = jnp.exp(scores - top_score)
    attn_probs = expo_terms / lax.optimization_barrier(jnp.sum(expo_terms, axis=-1, keepdims=True))
    context = jnp.einsum('hqk,khd->qhd', low(attn_probs), value_rows, precision=highest)
    context = low(low_back(context.reshape(row_count, HEADS * HEAD_DIM)))
    attended = low_back(matmul(context, w_output) + b_output)
    normed = layer_norm(inputs + attended, attn_gain, attn_shift)
    up_rows = low_back(matmul(low(normed), w_up) + b_up)
    down_rows = low_back(matmul(low(gelu_exact(up_rows)), w_down) + b_down)
    return layer_norm(normed + down_rows, ffn_gain, ffn_shift)

def reference(hidden_in, doc_ids, out_grad, w_query, b_query, w_key, w_value, b_value, w_output, b_output, attn_gain, attn_shift, w_up, b_up, w_down, b_down, ffn_gain, ffn_shift):
    params = tuple((weight.astype(jnp.float32) for weight in (w_query, b_query, w_key, w_value, b_value, w_output, b_output, attn_gain, attn_shift, w_up, b_up, w_down, b_down, ffn_gain, ffn_shift)))
    inputs = hidden_in.astype(jnp.float32).reshape(BLOCKS, ROWS, D)
    id_blocks = doc_ids.reshape(BLOCKS, ROWS)
    layer = jax.checkpoint(block_layer)

    def forward(weights, rows_in):
        return lax.map(lambda row_pair: layer(weights, row_pair[0], row_pair[1]), (rows_in, id_blocks))
    outputs, pullback = jax.vjp(forward, params, inputs)
    grad_params, grad_inputs = pullback(out_grad.astype(jnp.float32).reshape(BLOCKS, ROWS, D))
    g_wq, g_bq, g_wk, g_wv, g_bv, g_wo, g_bo, g_ga, g_sa, g_wu, g_bu, g_wd, g_bd, g_gf, g_sf = grad_params
    return (outputs.reshape(TOKENS, D).astype(jnp.bfloat16), grad_inputs.reshape(TOKENS, D), g_wq, g_bq, g_wk, g_wv, g_bv, g_wo, g_bo, g_ga, g_sa, g_wu, g_bu, g_wd, g_bd, g_gf, g_sf)
```

```python
import functools
import math

import jax
import jax.numpy as jnp
from jax import lax
from jax.sharding import PartitionSpec as P

D = 1024
HEADS = 16
HEAD_DIM = 64


norm_eps = 1e-12


def matmul(left, right):
    return jnp.dot(left, right, preferred_element_type=jnp.float32)


def matmul_tn(left, right):
    return lax.dot_general(
        left, right, (((0,), (0,)), ((), ())), preferred_element_type=jnp.float32
    )


def matmul_nt(left, right):
    return lax.dot_general(
        left, right, (((1,), (1,)), ((), ())), preferred_element_type=jnp.float32
    )


def layer_norm(values, gain, shift):
    centre = values - jnp.mean(values, axis=-1, keepdims=True)
    inverse = lax.rsqrt(jnp.mean(centre * centre, axis=-1, keepdims=True) + norm_eps)
    normed = centre * inverse
    return (normed * gain + shift, normed, inverse)


def norm_back(grad, normed, inverse):
    return inverse * (
        grad
        - jnp.mean(grad, axis=-1, keepdims=True)
        - normed * jnp.mean(grad * normed, axis=-1, keepdims=True)
    )


def gelu_exact(values):
    return 0.5 * values * (1.0 + jax.scipy.special.erf(values * (1.0 / math.sqrt(2.0))))


def gelu_slope(values):
    return 0.5 * (1.0 + jax.scipy.special.erf(values * (1.0 / math.sqrt(2.0)))) + values * jnp.exp(
        -0.5 * values * values
    ) * (1.0 / math.sqrt(2.0 * math.pi))


def masked_scores(queries, key_rows, allowed, score_scale):
    scores = (
        jnp.einsum("qhd,khd->hqk", queries, key_rows, preferred_element_type=jnp.float32)
        * score_scale
    )
    return jnp.where(allowed[None, :, :], scores, -1000000000.0)


def column_sum(values):
    return jnp.sum(values.astype(jnp.float32), axis=0)


AXES = ("wide", "ffn")


def hop(values, count, bit):
    return lax.ppermute(values, AXES, [(i, i ^ bit) for i in range(count)])


def gather_rows(shard, order, count, me):
    held = []
    buf = shard[None]
    for bit in order:
        got = hop(buf, count, bit)
        above = 2 ** sum(1 for other in held if other > bit)
        first = (me & bit) == 0
        low = jnp.where(first, buf, got).reshape((above, -1) + shard.shape)
        high = jnp.where(first, got, buf).reshape((above, -1) + shard.shape)
        buf = jnp.stack([low, high], axis=1).reshape((-1,) + shard.shape)
        held.append(bit)
    return buf


def scatter_sum(blocks, order, count, me):
    left = list(order)
    tail_shape = blocks.shape[1:]
    for bit in order:
        above = 2 ** sum(1 for other in left if other > bit)
        view = blocks.reshape((above, 2, -1) + tail_shape)
        mine = jnp.where((me & bit) == 0, 0, 1)
        keep = lax.dynamic_index_in_dim(view, mine, 1, keepdims=False)
        send = lax.dynamic_index_in_dim(view, 1 - mine, 1, keepdims=False)
        got = hop(send, count, bit)
        blocks = keep.astype(jnp.float32) + got.astype(jnp.float32)
        left.remove(bit)
        if left:
            blocks = blocks.astype(jnp.bfloat16)
        blocks = blocks.reshape((-1,) + tail_shape)
    return blocks[0]


def body(
    wide,
    ffn,
    hidden_in,
    doc_ids,
    out_grad,
    w_query,
    b_query,
    w_key,
    w_value,
    b_value,
    w_output,
    b_output,
    attn_gain,
    attn_shift,
    w_up,
    b_up,
    w_down,
    b_down,
    ffn_gain,
    ffn_shift,
):
    count = wide * ffn
    member = lax.axis_index("ffn")
    me = lax.axis_index("wide") * ffn + member
    far_bits = [1 << k for k in range(count.bit_length() - 1)][::-1]
    wide_bits = [bit for bit in far_bits if bit >= ffn]
    across, core = 2, 1
    order_a = wide_bits + [across, core]
    order_b = [across] + wide_bits + [core]
    order_c = wide_bits[:1] + wide_bits[2:] + [across] + wide_bits[1:2] + [core]
    order_up = wide_bits
    order_down = wide_bits[-1:] + wide_bits[:-1]
    low = jnp.bfloat16
    row_share = w_query.shape[0]
    up_columns = b_up.shape[0] // row_share

    vectors = (b_query, b_value, b_output, attn_gain, attn_shift, b_down, ffn_gain, ffn_shift)
    columns = jnp.concatenate(
        [jnp.stack(vectors, axis=0), b_up.reshape(up_columns, row_share)], axis=0
    ).T
    columns = jnp.pad(columns, ((0, 0), (0, 128 - columns.shape[1])))
    query_all = gather_rows(jnp.concatenate([w_query, columns], axis=1), order_a, count, me)
    key_full = gather_rows(w_key, order_b, count, me).reshape(D, D)
    value_full = gather_rows(w_value, order_c, count, me).reshape(D, D)
    query_full = query_all[:, :, :D].reshape(D, D)
    vector_rows = query_all[:, :, D:].reshape(D, 128).T.astype(jnp.float32)
    (
        bias_query,
        bias_value,
        bias_output,
        gain_one,
        shift_one,
        bias_down,
        gain_two,
        shift_two,
    ) = [vector_rows[k] for k in range(8)]
    bias_up_all = (
        vector_rows[8 : 8 + up_columns]
        .reshape(up_columns, count, row_share)
        .transpose(1, 0, 2)
        .reshape(-1)
    )
    w_output, w_up, w_down, _, _, _ = lax.optimization_barrier(
        (w_output, w_up, w_down, query_full, key_full, value_full)
    )
    output_full = gather_rows(w_output, order_b, count, me).reshape(D, D)
    up_part = gather_rows(w_up, order_up, count, me).reshape(D, -1)
    slice_len = up_part.shape[1]
    down_part = (
        gather_rows(w_down, order_down, count, me).transpose(1, 0, 2).reshape(slice_len, D)
    )

    row_count = hidden_in.shape[0]
    score_scale = HEAD_DIM ** (-0.5)
    residual_in = hidden_in.astype(jnp.float32)
    queries = (
        (matmul(hidden_in, query_full) + bias_query)
        .astype(jnp.bfloat16)
        .reshape(row_count, HEADS, HEAD_DIM)
    )
    key_rows = matmul(hidden_in, key_full).astype(jnp.bfloat16).reshape(row_count, HEADS, HEAD_DIM)
    value_rows = (
        (matmul(hidden_in, value_full) + bias_value)
        .astype(jnp.bfloat16)
        .reshape(row_count, HEADS, HEAD_DIM)
    )
    allowed = doc_ids[:, None] == doc_ids[None, :]
    scores = masked_scores(queries, key_rows, allowed, score_scale)
    top_score = jnp.max(scores, axis=-1, keepdims=True)
    expo_terms = jnp.exp(scores - top_score)
    total_sum = jnp.sum(expo_terms, axis=-1, keepdims=True)
    attn_probs = expo_terms / total_sum
    log_total = top_score + jnp.log(total_sum)
    context = (
        jnp.einsum(
            "hqk,khd->qhd",
            attn_probs.astype(jnp.bfloat16),
            value_rows,
            preferred_element_type=jnp.float32,
        )
        .reshape(row_count, D)
        .astype(jnp.bfloat16)
    )
    attended = matmul(context, output_full) + bias_output
    normed_out, normed_one, inverse_one = layer_norm(residual_in + attended, gain_one, shift_one)
    normed_low = normed_out.astype(jnp.bfloat16)
    bias_up = lax.dynamic_slice_in_dim(bias_up_all, member * slice_len, slice_len)

    def spread(rows):
        far = hop(rows, count, across)
        near = jnp.concatenate([rows, hop(rows, count, core)], axis=0)
        return near, jnp.concatenate([far, hop(far, count, core)], axis=0)

    def collect(near, far):
        near, far = near.astype(low), far.astype(low)
        there = far[:row_count].astype(jnp.float32) + hop(far[row_count:], count, core).astype(
            jnp.float32
        )
        there = hop(there.astype(low), count, across).astype(jnp.float32)
        here = near[:row_count].astype(jnp.float32) + hop(near[row_count:], count, core).astype(
            jnp.float32
        )
        return here + there

    rows_near, rows_far = spread(normed_low)
    up_near = matmul(rows_near, up_part) + bias_up
    up_far = matmul(rows_far, up_part) + bias_up
    active_near = gelu_exact(up_near).astype(jnp.bfloat16)
    active_far = gelu_exact(up_far).astype(jnp.bfloat16)
    down_rows = (
        collect(matmul(active_near, down_part), matmul(active_far, down_part)) + bias_down
    )
    layer_out, normed_two, inverse_two = layer_norm(normed_out + down_rows, gain_two, shift_two)
    grad_out = out_grad.astype(jnp.float32)
    grad_gain_two = jnp.sum(grad_out * normed_two, axis=0)
    grad_shift_two = jnp.sum(grad_out, axis=0)
    grad_two = norm_back(grad_out * gain_two, normed_two, inverse_two)
    grad_two_low = grad_two.astype(jnp.bfloat16)
    grad_bias_down = column_sum(grad_two_low)
    grad_near, grad_far = spread(grad_two_low)
    grad_up_near = (matmul_nt(grad_near, down_part) * gelu_slope(up_near)).astype(jnp.bfloat16)
    grad_up_far = (matmul_nt(grad_far, down_part) * gelu_slope(up_far)).astype(jnp.bfloat16)
    grad_one = grad_two + collect(
        matmul_nt(grad_up_near, up_part), matmul_nt(grad_up_far, up_part)
    )
    grad_up_all = jnp.concatenate([grad_up_near, grad_up_far], axis=0)
    grad_bias_up = lax.dynamic_update_slice_in_dim(
        jnp.zeros(bias_up_all.shape, jnp.float32), column_sum(grad_up_all), member * slice_len, 0
    )
    grad_up_w = matmul_tn(jnp.concatenate([rows_near, rows_far], axis=0), grad_up_all).astype(low)
    grad_down_w = matmul_tn(
        jnp.concatenate([active_near, active_far], axis=0),
        jnp.concatenate([grad_near, grad_far], axis=0),
    ).astype(low)
    grad_up_w = scatter_sum(grad_up_w.reshape(wide, -1, slice_len), order_up[::-1], count, me)
    grad_down_w = scatter_sum(
        grad_down_w.reshape(slice_len, wide, -1).transpose(1, 0, 2), order_down[::-1], count, me
    )
    grad_gain_one = jnp.sum(grad_one * normed_one, axis=0)
    grad_shift_one = jnp.sum(grad_one, axis=0)
    grad_z_one = norm_back(grad_one * gain_one, normed_one, inverse_one)
    grad_att_low = grad_z_one.astype(jnp.bfloat16)
    grad_bias_output = column_sum(grad_att_low)

    def share_out(full, order):
        return scatter_sum(
            full.astype(low).reshape(count, row_share, -1), order[::-1], count, me
        )

    grad_output_w = share_out(matmul_tn(context, grad_att_low), order_b)
    grad_context = (
        matmul_nt(grad_att_low, output_full)
        .astype(jnp.bfloat16)
        .reshape(row_count, HEADS, HEAD_DIM)
    )
    scores = masked_scores(queries, key_rows, allowed, score_scale)
    attn_probs = jnp.exp(scores - log_total)
    grad_probs = jnp.einsum(
        "qhd,khd->hqk", grad_context, value_rows, preferred_element_type=jnp.float32
    )
    grad_values = (
        jnp.einsum(
            "hqk,qhd->khd",
            attn_probs.astype(jnp.bfloat16),
            grad_context,
            preferred_element_type=jnp.float32,
        )
        .astype(jnp.bfloat16)
        .reshape(row_count, D)
    )
    row_inner = jnp.sum(attn_probs * grad_probs, axis=-1, keepdims=True)
    grad_scores = (attn_probs * (grad_probs - row_inner)).astype(jnp.bfloat16)
    grad_queries = (
        (
            jnp.einsum("hqk,khd->qhd", grad_scores, key_rows, preferred_element_type=jnp.float32)
            * score_scale
        )
        .astype(jnp.bfloat16)
        .reshape(row_count, D)
    )
    grad_keys = (
        (
            jnp.einsum("hqk,qhd->khd", grad_scores, queries, preferred_element_type=jnp.float32)
            * score_scale
        )
        .astype(jnp.bfloat16)
        .reshape(row_count, D)
    )
    grad_value_w = share_out(matmul_tn(hidden_in, grad_values), order_c)
    grad_key_w = share_out(matmul_tn(hidden_in, grad_keys), order_b)
    sums = jnp.stack(
        [
            column_sum(grad_queries),
            column_sum(grad_values),
            grad_bias_output,
            grad_gain_one,
            grad_shift_one,
            grad_bias_down,
            grad_gain_two,
            grad_shift_two,
        ],
        axis=0,
    )
    sums_up = grad_bias_up.reshape(count, up_columns, row_share).transpose(1, 0, 2)
    sums = jnp.concatenate([sums, sums_up.reshape(up_columns, D)], axis=0).T
    sums = jnp.pad(sums, ((0, 0), (0, 128 - sums.shape[1]))).astype(low)
    grad_query_all = share_out(
        jnp.concatenate([matmul_tn(hidden_in, grad_queries).astype(low), sums], axis=1), order_a
    )
    grad_query_w = grad_query_all[:, :D]
    summed = grad_query_all[:, D:].T
    grad_input = (
        grad_z_one
        + matmul_nt(grad_queries, query_full)
        + matmul_nt(grad_keys, key_full)
        + matmul_nt(grad_values, value_full)
    )
    return (
        layer_out.astype(jnp.bfloat16),
        grad_input,
        grad_query_w,
        summed[0],
        grad_key_w,
        grad_value_w,
        summed[1],
        grad_output_w,
        summed[2],
        summed[3],
        summed[4],
        grad_up_w,
        summed[8 : 8 + up_columns].reshape(-1),
        grad_down_w,
        summed[5],
        summed[6],
        summed[7],
    )


def solution(mesh):
    in_specs = (
        P(("wide", "ffn"), None),
        P(("wide", "ffn")),
        P(("wide", "ffn"), None),
        P(("wide", "ffn"), None),
        P(("wide", "ffn")),
        P(("wide", "ffn"), None),
        P(("wide", "ffn"), None),
        P(("wide", "ffn")),
        P(("wide", "ffn"), None),
        P(("wide", "ffn")),
        P(("wide", "ffn")),
        P(("wide", "ffn")),
        P("wide", "ffn"),
        P(("wide", "ffn")),
        P("ffn", "wide"),
        P(("wide", "ffn")),
        P(("wide", "ffn")),
        P(("wide", "ffn")),
    )
    out_specs = (
        P(("wide", "ffn"), None),
        P(("wide", "ffn"), None),
        P(("wide", "ffn"), None),
        P(("wide", "ffn")),
        P(("wide", "ffn"), None),
        P(("wide", "ffn"), None),
        P(("wide", "ffn")),
        P(("wide", "ffn"), None),
        P(("wide", "ffn")),
        P(("wide", "ffn")),
        P(("wide", "ffn")),
        P("wide", "ffn"),
        P(("wide", "ffn")),
        P("ffn", "wide"),
        P(("wide", "ffn")),
        P(("wide", "ffn")),
        P(("wide", "ffn")),
    )
    return jax.shard_map(
        functools.partial(body, mesh.shape["wide"], mesh.shape["ffn"]), mesh=mesh, in_specs=in_specs, out_specs=out_specs, check_vma=False)
```

```python
import functools
import math

import jax
import jax.numpy as jnp
from jax import lax
from jax.sharding import PartitionSpec as P

D = 1024
HEADS = 16
HEAD_DIM = 64


norm_eps = 1e-12


def matmul(left, right):
    return jnp.dot(left, right, preferred_element_type=jnp.float32)


def matmul_tn(left, right):
    return lax.dot_general(
        left, right, (((0,), (0,)), ((), ())), preferred_element_type=jnp.float32
    )


def matmul_nt(left, right):
    return lax.dot_general(
        left, right, (((1,), (1,)), ((), ())), preferred_element_type=jnp.float32
    )


def layer_norm(values, gain, shift):
    centre = values - jnp.mean(values, axis=-1, keepdims=True)
    inverse = lax.rsqrt(jnp.mean(centre * centre, axis=-1, keepdims=True) + norm_eps)
    normed = centre * inverse
    return (normed * gain + shift, normed, inverse)


def norm_back(grad, normed, inverse):
    return inverse * (
        grad
        - jnp.mean(grad, axis=-1, keepdims=True)
        - normed * jnp.mean(grad * normed, axis=-1, keepdims=True)
    )


def gelu_exact(values):
    return 0.5 * values * (1.0 + jax.scipy.special.erf(values * (1.0 / math.sqrt(2.0))))


def gelu_slope(values):
    return 0.5 * (1.0 + jax.scipy.special.erf(values * (1.0 / math.sqrt(2.0)))) + values * jnp.exp(
        -0.5 * values * values
    ) * (1.0 / math.sqrt(2.0 * math.pi))


def masked_scores(queries, key_rows, allowed, score_scale):
    scores = (
        jnp.einsum("qhd,khd->hqk", queries, key_rows, preferred_element_type=jnp.float32)
        * score_scale
    )
    return jnp.where(allowed[None, :, :], scores, -1000000000.0)


def column_sum(values):
    return jnp.sum(values.astype(jnp.float32), axis=0)


AXES = ("wide", "ffn")


def hop(values, count, bit):
    return lax.ppermute(values, AXES, [(i, i ^ bit) for i in range(count)])


def after(value, *others):
    return lax.optimization_barrier((value,) + others)[0]


def gather_steps(buf, held, order, count, me):
    held = list(held)
    block = buf.shape[1:]
    for bit in order:
        got = hop(buf, count, bit)
        above = 2 ** sum(1 for other in held if other > bit)
        first = (me & bit) == 0
        low = jnp.where(first, buf, got).reshape((above, -1) + block)
        high = jnp.where(first, got, buf).reshape((above, -1) + block)
        buf = jnp.stack([low, high], axis=1).reshape((-1,) + block)
        held.append(bit)
    return buf


def scatter_sum(blocks, order, count, me):
    left = list(order)
    tail_shape = blocks.shape[1:]
    for bit in order:
        above = 2 ** sum(1 for other in left if other > bit)
        view = blocks.reshape((above, 2, -1) + tail_shape)
        mine = jnp.where((me & bit) == 0, 0, 1)
        keep = lax.dynamic_index_in_dim(view, mine, 1, keepdims=False)
        send = lax.dynamic_index_in_dim(view, 1 - mine, 1, keepdims=False)
        got = hop(send, count, bit)
        blocks = keep.astype(jnp.float32) + got.astype(jnp.float32)
        left.remove(bit)
        if left:
            blocks = blocks.astype(jnp.bfloat16)
        blocks = blocks.reshape((-1,) + tail_shape)
    return blocks[0]


def body(
    wide,
    ffn,
    hidden_in,
    doc_ids,
    out_grad,
    w_query,
    b_query,
    w_key,
    w_value,
    b_value,
    w_output,
    b_output,
    attn_gain,
    attn_shift,
    w_up,
    b_up,
    w_down,
    b_down,
    ffn_gain,
    ffn_shift,
):
    count = wide * ffn
    member = lax.axis_index("ffn")
    me = lax.axis_index("wide") * ffn + member
    far_bits = [1 << k for k in range(count.bit_length() - 1)][::-1]
    wide_bits = [bit for bit in far_bits if bit >= ffn]
    across, core = 2, 1
    order_a = wide_bits + [across, core]
    order_b = [across] + wide_bits + [core]
    order_c = wide_bits[:1] + wide_bits[2:] + [across] + wide_bits[1:2] + [core]
    order_o = wide_bits[-1:] + wide_bits[:-1] + [across, core]
    low = jnp.bfloat16
    row_share = w_query.shape[0]
    up_columns = b_up.shape[0] // row_share

    vectors = (b_query, b_value, b_output, attn_gain, attn_shift, b_down, ffn_gain, ffn_shift)
    columns = jnp.concatenate(
        [jnp.stack(vectors, axis=0), b_up.reshape(up_columns, row_share)], axis=0
    ).T
    columns = jnp.pad(columns, ((0, 0), (0, 128 - columns.shape[1])))
    query_buf = jnp.concatenate([w_query, columns], axis=1)[None]
    query_buf = gather_steps(query_buf, [], order_a[:2], count, me)
    up_buf = after(w_up, query_buf)[None]
    up_buf = gather_steps(up_buf, [], wide_bits[:-1], count, me)
    down_buf = after(w_down.T, up_buf)[None]
    query_buf = gather_steps(query_buf, order_a[:2], order_a[2:-1], count, me)
    key_buf = gather_steps(w_key[None], [], order_b[:-1], count, me)
    value_buf = gather_steps(w_value[None], [], order_c[:-1], count, me)
    output_buf = after(w_output, query_buf)[None]
    query_all = gather_steps(query_buf, order_a[:-1], [core], count, me)
    key_full = gather_steps(key_buf, order_b[:-1], [core], count, me).reshape(D, D)
    value_full = gather_steps(value_buf, order_c[:-1], [core], count, me).reshape(D, D)
    query_full = query_all[:, :, :D].reshape(D, D)
    vector_rows = query_all[:, :, D:].reshape(D, 128).T.astype(jnp.float32)
    (
        bias_query,
        bias_value,
        bias_output,
        gain_one,
        shift_one,
        bias_down,
        gain_two,
        shift_two,
    ) = [vector_rows[k] for k in range(8)]
    bias_up_all = (
        vector_rows[8 : 8 + up_columns]
        .reshape(up_columns, count, row_share)
        .transpose(1, 0, 2)
        .reshape(-1)
    )
    output_full = gather_steps(output_buf, [], order_o, count, me).reshape(D, D)
    up_part = gather_steps(up_buf, wide_bits[:-1], wide_bits[-1:], count, me).reshape(D, -1)
    down_part = gather_steps(down_buf, [], wide_bits, count, me).reshape(D, -1)
    slice_len = up_part.shape[1]

    row_count = hidden_in.shape[0]
    score_scale = HEAD_DIM ** (-0.5)
    residual_in = hidden_in.astype(jnp.float32)
    queries = (
        (matmul(hidden_in, query_full) + bias_query)
        .astype(jnp.bfloat16)
        .reshape(row_count, HEADS, HEAD_DIM)
    )
    key_rows = matmul(hidden_in, key_full).astype(jnp.bfloat16).reshape(row_count, HEADS, HEAD_DIM)
    value_rows = (
        (matmul(hidden_in, value_full) + bias_value)
        .astype(jnp.bfloat16)
        .reshape(row_count, HEADS, HEAD_DIM)
    )
    allowed = doc_ids[:, None] == doc_ids[None, :]
    scores = masked_scores(queries, key_rows, allowed, score_scale)
    top_score = jnp.max(scores, axis=-1, keepdims=True)
    expo_terms = jnp.exp(scores - top_score)
    total_sum = jnp.sum(expo_terms, axis=-1, keepdims=True)
    attn_probs = expo_terms / total_sum
    log_total = top_score + jnp.log(total_sum)
    context = (
        jnp.einsum(
            "hqk,khd->qhd",
            attn_probs.astype(jnp.bfloat16),
            value_rows,
            preferred_element_type=jnp.float32,
        )
        .reshape(row_count, D)
        .astype(jnp.bfloat16)
    )
    attended = matmul(context, output_full) + bias_output
    normed_out, normed_one, inverse_one = layer_norm(residual_in + attended, gain_one, shift_one)
    normed_low = normed_out.astype(jnp.bfloat16)
    bias_up = lax.dynamic_slice_in_dim(bias_up_all, member * slice_len, slice_len)

    def spread(rows):
        far = hop(rows, count, across)
        near = jnp.concatenate([rows, hop(rows, count, core)], axis=0)
        return near, jnp.concatenate([far, hop(far, count, core)], axis=0)

    def collect(near, far):
        near, far = near.astype(low), far.astype(low)
        there = far[:row_count].astype(jnp.float32) + hop(far[row_count:], count, core).astype(
            jnp.float32
        )
        leaving = there.astype(low)
        there = hop(leaving, count, across).astype(jnp.float32)
        here = near[:row_count].astype(jnp.float32) + hop(near[row_count:], count, core).astype(
            jnp.float32
        )
        return here + there, leaving

    rows_near, rows_far = spread(normed_low)
    up_near = matmul(rows_near, up_part) + bias_up
    up_far = matmul(rows_far, up_part) + bias_up
    active_near = gelu_exact(up_near).astype(jnp.bfloat16)
    active_far = gelu_exact(up_far).astype(jnp.bfloat16)
    down_rows = (
        collect(matmul_nt(active_near, down_part), matmul_nt(active_far, down_part))[0] + bias_down
    )
    layer_out, normed_two, inverse_two = layer_norm(normed_out + down_rows, gain_two, shift_two)
    grad_out = out_grad.astype(jnp.float32)
    grad_gain_two = jnp.sum(grad_out * normed_two, axis=0)
    grad_shift_two = jnp.sum(grad_out, axis=0)
    grad_two = norm_back(grad_out * gain_two, normed_two, inverse_two)
    grad_two_low = grad_two.astype(jnp.bfloat16)
    grad_bias_down = column_sum(grad_two_low)
    grad_near, grad_far = spread(grad_two_low)
    grad_up_near = (matmul(grad_near, down_part) * gelu_slope(up_near)).astype(jnp.bfloat16)
    grad_up_far = (matmul(grad_far, down_part) * gelu_slope(up_far)).astype(jnp.bfloat16)
    collected, leaving = collect(
        matmul_nt(grad_up_near, up_part), matmul_nt(grad_up_far, up_part)
    )
    grad_one = grad_two + collected
    rows_near, grad_near, _ = lax.optimization_barrier((rows_near, grad_near, leaving))
    grad_up_all = jnp.concatenate([grad_up_near, grad_up_far], axis=0)
    grad_bias_up = lax.dynamic_update_slice_in_dim(
        jnp.zeros(bias_up_all.shape, jnp.float32), column_sum(grad_up_all), member * slice_len, 0
    )
    grad_down_w = matmul_tn(
        jnp.concatenate([grad_near, grad_far], axis=0),
        jnp.concatenate([active_near, active_far], axis=0),
    ).astype(low)
    grad_up_w = matmul_tn(jnp.concatenate([rows_near, rows_far], axis=0), grad_up_all).astype(low)
    grad_down_w = scatter_sum(
        grad_down_w.reshape(wide, -1, slice_len), wide_bits[::-1], count, me
    ).T
    grad_up_w = scatter_sum(grad_up_w.reshape(wide, -1, slice_len), wide_bits[::-1], count, me)
    grad_gain_one = jnp.sum(grad_one * normed_one, axis=0)
    grad_shift_one = jnp.sum(grad_one, axis=0)
    grad_z_one = norm_back(grad_one * gain_one, normed_one, inverse_one)
    grad_att_low = grad_z_one.astype(jnp.bfloat16)
    grad_bias_output = column_sum(grad_att_low)

    half = count // 2

    def both_cores(rows):
        return jnp.concatenate([rows, hop(rows, count, core)], axis=0)

    def kept_columns(rows):
        view = both_cores(rows).reshape(2 * row_count, half, 2, row_share)
        kept = lax.dynamic_index_in_dim(view, me & core, 2, keepdims=False)
        return kept.reshape(2 * row_count, half * row_share)

    def share_out(full, order):
        return scatter_sum(full.reshape(half, row_share, -1), order[::-1][1:], count, me)

    hidden_kept = kept_columns(hidden_in)
    grad_output_w = share_out(
        matmul_tn(kept_columns(context), both_cores(grad_att_low)).astype(low), order_o
    )
    grad_context = (
        matmul_nt(grad_att_low, output_full)
        .astype(jnp.bfloat16)
        .reshape(row_count, HEADS, HEAD_DIM)
    )
    scores = masked_scores(queries, key_rows, allowed, score_scale)
    attn_probs = jnp.exp(scores - log_total)
    grad_probs = jnp.einsum(
        "qhd,khd->hqk", grad_context, value_rows, preferred_element_type=jnp.float32
    )
    grad_values = (
        jnp.einsum(
            "hqk,qhd->khd",
            attn_probs.astype(jnp.bfloat16),
            grad_context,
            preferred_element_type=jnp.float32,
        )
        .astype(jnp.bfloat16)
        .reshape(row_count, D)
    )
    row_inner = jnp.sum(attn_probs * grad_probs, axis=-1, keepdims=True)
    grad_scores = (attn_probs * (grad_probs - row_inner)).astype(jnp.bfloat16)
    grad_queries = (
        (
            jnp.einsum("hqk,khd->qhd", grad_scores, key_rows, preferred_element_type=jnp.float32)
            * score_scale
        )
        .astype(jnp.bfloat16)
        .reshape(row_count, D)
    )
    grad_keys = (
        (
            jnp.einsum("hqk,qhd->khd", grad_scores, queries, preferred_element_type=jnp.float32)
            * score_scale
        )
        .astype(jnp.bfloat16)
        .reshape(row_count, D)
    )
    grad_value_w = share_out(
        matmul_tn(hidden_kept, both_cores(grad_values)).astype(low), order_c
    )
    grad_key_w = share_out(
        matmul_tn(hidden_kept, both_cores(grad_keys)).astype(low), order_b
    )
    sums = jnp.stack(
        [
            column_sum(grad_queries),
            column_sum(grad_values),
            grad_bias_output,
            grad_gain_one,
            grad_shift_one,
            grad_bias_down,
            grad_gain_two,
            grad_shift_two,
        ],
        axis=0,
    )
    sums_up = grad_bias_up.reshape(count, up_columns, row_share).transpose(1, 0, 2)
    sums = jnp.concatenate([sums, sums_up.reshape(up_columns, D)], axis=0).T
    sums = jnp.pad(sums, ((0, 0), (0, 128 - sums.shape[1]))).reshape(half, 2, row_share, 128)
    sums_kept = lax.dynamic_index_in_dim(sums, me & core, 1, keepdims=False)
    sums_sent = lax.dynamic_index_in_dim(sums, 1 - (me & core), 1, keepdims=False)
    sums = sums_kept + hop(sums_sent.astype(low), count, core).astype(jnp.float32)
    sums = sums.reshape(half * row_share, 128).astype(low)
    grad_query_all = share_out(
        jnp.concatenate(
            [matmul_tn(hidden_kept, both_cores(grad_queries)).astype(low), sums], axis=1
        ),
        order_a,
    )
    grad_query_w = grad_query_all[:, :D]
    summed = grad_query_all[:, D:].T
    grad_input = (
        grad_z_one
        + matmul_nt(grad_queries, query_full)
        + matmul_nt(grad_keys, key_full)
        + matmul_nt(grad_values, value_full)
    )
    return (
        layer_out.astype(jnp.bfloat16),
        grad_input,
        grad_query_w,
        summed[0],
        grad_key_w,
        grad_value_w,
        summed[1],
        grad_output_w,
        summed[2],
        summed[3],
        summed[4],
        grad_up_w,
        summed[8 : 8 + up_columns].reshape(-1),
        grad_down_w,
        summed[5],
        summed[6],
        summed[7],
    )


def solution(mesh):
    in_specs = (
        P(("wide", "ffn"), None),
        P(("wide", "ffn")),
        P(("wide", "ffn"), None),
        P(("wide", "ffn"), None),
        P(("wide", "ffn")),
        P(("wide", "ffn"), None),
        P(("wide", "ffn"), None),
        P(("wide", "ffn")),
        P(("wide", "ffn"), None),
        P(("wide", "ffn")),
        P(("wide", "ffn")),
        P(("wide", "ffn")),
        P("wide", "ffn"),
        P(("wide", "ffn")),
        P("ffn", "wide"),
        P(("wide", "ffn")),
        P(("wide", "ffn")),
        P(("wide", "ffn")),
    )
    out_specs = (
        P(("wide", "ffn"), None),
        P(("wide", "ffn"), None),
        P(("wide", "ffn"), None),
        P(("wide", "ffn")),
        P(("wide", "ffn"), None),
        P(("wide", "ffn"), None),
        P(("wide", "ffn")),
        P(("wide", "ffn"), None),
        P(("wide", "ffn")),
        P(("wide", "ffn")),
        P(("wide", "ffn")),
        P("wide", "ffn"),
        P(("wide", "ffn")),
        P("ffn", "wide"),
        P(("wide", "ffn")),
        P(("wide", "ffn")),
        P(("wide", "ffn")),
    )
    return jax.shard_map(
        functools.partial(body, mesh.shape["wide"], mesh.shape["ffn"]), mesh=mesh, in_specs=in_specs, out_specs=out_specs, check_vma=False)
```
